32 devices in a mesh: dp: 8 (over z, x), tensor: 4 (over y, core).
Axes of the slice: x: 2, y: 2, z: 4, core: 2. Of those that a mesh axis runs over, the one named last changes fastest.
Arguments:
- layer_in: bfloat16 [4096, 2048], P(('dp', 'tensor')), may hold values from -6 to 6
- positions: int32 [4096], P('dp'), may hold values from 0 to 511, as said below
- attn_gain: bfloat16 [2048], P('dp'), may hold values from 0.5 to 1.5
- w_query: bfloat16 [2048, 2048], P('dp', 'tensor'), may hold values from -3.6239223 to 3.6239223
- w_key: bfloat16 [2048, 512], P('dp', 'tensor'), may hold values from -0.088388348 to 0.088388348
- w_value: bfloat16 [2048, 512], P('dp', 'tensor'), may hold values from -0.125 to 0.125
- w_out: bfloat16 [2048, 2048], P('tensor', 'dp'), may hold values from -0.5 to 0.5
- mlp_gain: bfloat16 [2048], P('dp'), may hold values from 0.5 to 1.5
- w_gate: bfloat16 [2048, 8192], P('dp', 'tensor'), may hold values from -0.125 to 0.125
- w_up: bfloat16 [2048, 8192], P('dp', 'tensor'), may hold values from -0.125 to 0.125
- w_down: bfloat16 [8192, 2048], P('tensor', 'dp'), may hold values from -0.0625 to 0.0625
- grad_out: bfloat16 [4096, 2048], P(('dp', 'tensor')), may hold values from -6 to 6
Outputs:
- layer_out: bfloat16 [4096, 2048], P(('dp', 'tensor'))
- grad_in: float32 [4096, 2048], P(('dp', 'tensor'))
- grad_attn_gain: float32 [2048], P('dp')
- grad_query: float32 [2048, 2048], P('dp', 'tensor')
- grad_key: float32 [2048, 512], P('dp', 'tensor')
- grad_value: float32 [2048, 512], P('dp', 'tensor')
- grad_attn_out: float32 [2048, 2048], P('tensor', 'dp')
- grad_mlp_gain: float32 [2048], P('dp')
- grad_gate: float32 [2048, 8192], P('dp', 'tensor')
- grad_up: float32 [2048, 8192], P('dp', 'tensor')
- grad_down: float32 [8192, 2048], P('tensor', 'dp')
The draws below stay inside these ranges and needn't reach their ends.
Inputs may be any that keep to these rules, and one draw needn't show every extreme that they name: Each sequence of 512 tokens is cut into documents; positions count from 0 at a document's first token and rise by one a token; every sequence starts at position 0.
All inputs are finite; a program needn't handle non-finite values.
Results may differ from the reference program's by a relative error of at most 0.014.
Values may be sent and summed in bfloat16 or wider, within the bound.
No kernel may reach another device: no remote copies, remote signals or barrier semaphores. Data moves between devices by JAX's collectives and lax.ppermute only.
A program may use at most 192 MiB of HBM per device.

```python
import jax
import jax.numpy as jnp
from jax import lax

D = 2048
H = 32
KV = 8
HD = 64
FF = 8192
LEN = 512
TOKENS = 4096
N_DP = 8


def key_matrix(key):
    raw = jax.random.normal(jax.random.fold_in(key, 71), (D, KV * HD), jnp.float32)
    return jnp.clip(raw, -4.0, 4.0) * D ** (-0.5)


def draw_w_key(key, part):
    return key_matrix(key).astype(jnp.bfloat16)


def draw_w_query(key, part):
    raw = jax.random.normal(jax.random.fold_in(key, 13), (D, H * HD), jnp.float32)
    base = jnp.clip(raw, -4.0, 4.0) * D ** (-0.5)
    return base.astype(jnp.bfloat16)


def draw_positions(key, part):
    sequences = TOKENS // LEN
    draws = jax.random.randint(jax.random.fold_in(key, 5), (sequences, LEN), 0, LEN)
    token_index = jnp.arange(LEN, dtype=jnp.int32)[None, :]
    seq_index = jnp.arange(sequences, dtype=jnp.int32)[:, None]
    whole_seq = jax.random.randint(jax.random.fold_in(key, 9), (), 0, sequences)
    boundary = (draws < 3) | (token_index == 0)
    boundary = jnp.where(seq_index == whole_seq, token_index == 0, boundary)
    begins = lax.cummax(jnp.where(boundary, token_index, 0), axis=1)
    return (token_index - begins).reshape(TOKENS).astype(jnp.int32)


def level_of(own_key, extent, pieces, least, largest):
    factor_of, own = 1.0, jax.random.fold_in(own_key, 6)
    for dim, blocks in pieces:
        steps = jnp.exp(jax.random.uniform(jax.random.fold_in(own, dim), (blocks,), jnp.float32, least / len(pieces), largest / len(pieces)))
        factor_of = factor_of * jnp.repeat(steps, extent[dim] // blocks).reshape([-1 if axis == dim else 1 for axis in range(len(extent))])
    return factor_of


def noise(own_key, dims, scale, limit, shards=(), held_as=jnp.bfloat16):
    entries = jax.random.normal(own_key, dims, jnp.float32) * scale
    if len(shards) > 0:
        entries = level_of(own_key, dims, shards, -0.22, 0.18) * entries
    return jnp.clip(entries, min=-limit, max=limit).astype(held_as)


def setup_inputs(seed: int = 0) -> dict:
    streams_of = jax.random.split(jax.random.key(seed), 13)
    return {
        "layer_in": noise(streams_of[0], (TOKENS, D), 1.0, 6.0, ((0, 32),)),
        "positions": draw_positions(jax.random.fold_in(streams_of[12], 71), 0),
        "attn_gain": jnp.clip(1.0 + 0.1 * jax.random.normal(streams_of[2], (D,), jnp.float32), 0.5, 1.5).astype(jnp.bfloat16),
        "w_query": draw_w_query(jax.random.fold_in(streams_of[12], 71), 0),
        "w_key": draw_w_key(jax.random.fold_in(streams_of[12], 71), 0),
        "w_value": noise(streams_of[5], (D, KV * HD), D ** -0.5, 0.125, ((0, 8), (1, 4))),
        "w_out": noise(streams_of[6], (H * HD, D), (H * HD // 16) ** -0.5, 0.5, ((0, 4), (1, 8))),
        "mlp_gain": jnp.clip(1.0 + 0.1 * jax.random.normal(streams_of[7], (D,), jnp.float32), 0.5, 1.5).astype(jnp.bfloat16),
        "w_gate": noise(streams_of[8], (D, FF), D ** -0.5, 0.125, ((0, 8), (1, 4))),
        "w_up": noise(streams_of[9], (D, FF), D ** -0.5, 0.125, ((0, 8), (1, 4))),
        "w_down": noise(streams_of[10], (FF, D), FF ** -0.5, 0.0625, ((0, 4), (1, 8))),
        "grad_out": noise(streams_of[11], (TOKENS, D), 1.0, 6.0, ((0, 32),)),
    }


epsilon = 1e-05
rope_base = 500000.0

def matmul(left, right):
    return jnp.dot(left, right, preferred_element_type=jnp.float32)

def outer_product(left, right):
    return lax.dot_general(left, right, (((0,), (0,)), ((), ())), preferred_element_type=jnp.float32)

def times_transpose(left, right):
    return lax.dot_general(left, right, (((1,), (1,)), ((), ())), preferred_element_type=jnp.float32)

def widen(values):
    return lax.optimization_barrier(values).astype(jnp.float32)

def rotary_tables(positions, head_size):
    half_width = head_size // 2
    inverse = rope_base ** (-2.0 * jnp.arange(half_width, dtype=jnp.float32) / head_size)
    angles = positions.astype(jnp.float32)[:, None] * inverse[None, :]
    return (jnp.cos(angles), jnp.sin(angles))

def rotate(vectors, cosine_table, sine_table):
    half_width = vectors.shape[-1] // 2
    front_half = vectors[..., :half_width]
    back_half = vectors[..., half_width:]
    cosine = cosine_table[:, None, :]
    sine_part = sine_table[:, None, :]
    return jnp.concatenate([front_half * cosine - back_half * sine_part, back_half * cosine + front_half * sine_part], axis=-1)

def unrotate(vectors, cosine_table, sine_table):
    half_width = vectors.shape[-1] // 2
    front_half = vectors[..., :half_width]
    back_half = vectors[..., half_width:]
    cosine = cosine_table[:, None, :]
    sine_part = sine_table[:, None, :]
    return jnp.concatenate([front_half * cosine + back_half * sine_part, back_half * cosine - front_half * sine_part], axis=-1)

def norm_backward(grad_normed, normed, inverse_rms):
    return inverse_rms * (grad_normed - normed * lax.optimization_barrier(jnp.mean(grad_normed * normed, axis=-1, keepdims=True)))

def masked_scores(query_block, key_wide, doc_starts, block_id, block_rows):
    length = key_wide.shape[0]
    token_index = jnp.arange(length, dtype=jnp.int32)
    row_index = block_id * block_rows + jnp.arange(block_rows, dtype=jnp.int32)
    row_starts = lax.dynamic_slice_in_dim(doc_starts, block_id * block_rows, block_rows, 0)
    allowed = (token_index[None, :] <= row_index[:, None]) & (doc_starts[None, :] == row_starts[:, None])
    scores = jnp.einsum('rkgd,lkd->kgrl', widen(query_block), key_wide)
    scores = scores * query_block.shape[-1] ** (-0.5)
    return jnp.where(allowed[None, None], scores, -jnp.inf)

def attend(queries, key_rows, value_rows, doc_starts):
    length = queries.shape[0]
    block_rows = min(512, length)
    blocks = length // block_rows
    key_wide = widen(key_rows)
    value_wide = widen(value_rows)

    def per_block(block_id):
        query_block = lax.dynamic_slice_in_dim(queries, block_id * block_rows, block_rows, 0)
        scores = masked_scores(query_block, key_wide, doc_starts, block_id, block_rows)
        row_max = lax.optimization_barrier(jnp.max(scores, axis=-1, keepdims=True))
        exponent = jnp.exp(scores - row_max)
        row_total = lax.optimization_barrier(jnp.sum(exponent, axis=-1, keepdims=True))
        probabilities = (exponent / row_total).astype(jnp.bfloat16)
        mixed_rows = jnp.einsum('kgrl,lkd->rkgd', widen(probabilities), value_wide)
        return (mixed_rows.astype(jnp.bfloat16), (row_max + jnp.log(row_total))[..., 0])
    mixed_rows, log_totals = lax.map(per_block, jnp.arange(blocks, dtype=jnp.int32))
    return (mixed_rows.reshape(queries.shape), log_totals)

def attend_back(queries, key_rows, value_rows, grad_mixed, log_totals, doc_starts):
    length = queries.shape[0]
    head_size = queries.shape[-1]
    block_rows = min(512, length)
    blocks = length // block_rows
    score_scale = head_size ** (-0.5)
    key_wide = widen(key_rows)
    value_wide = widen(value_rows)

    def per_block(carry, block_id):
        key_grad, value_grad = carry
        query_block = lax.dynamic_slice_in_dim(queries, block_id * block_rows, block_rows, 0)
        grad_block = widen(lax.dynamic_slice_in_dim(grad_mixed, block_id * block_rows, block_rows, 0))
        total_block = log_totals[block_id]
        scores = masked_scores(query_block, key_wide, doc_starts, block_id, block_rows)
        probabilities = jnp.exp(scores - total_block[..., None])
        prob_rounded = widen(probabilities.astype(jnp.bfloat16))
        grad_prob = jnp.einsum('rkgd,lkd->kgrl', grad_block, value_wide)
        row_delta = lax.optimization_barrier(jnp.sum(probabilities * grad_prob, axis=-1, keepdims=True))
        grad_score = widen((probabilities * (grad_prob - row_delta)).astype(jnp.bfloat16))
        query_grad = jnp.einsum('kgrl,lkd->rkgd', grad_score, key_wide) * score_scale
        key_grad = key_grad + jnp.einsum('kgrl,rkgd->lkd', grad_score, widen(query_block)) * score_scale
        value_grad = value_grad + jnp.einsum('kgrl,rkgd->lkd', prob_rounded, grad_block)
        return ((key_grad, value_grad), query_grad)
    zeros_rows = jnp.zeros(key_rows.shape, jnp.float32)
    (key_grad, value_grad), query_grad = lax.scan(per_block, (zeros_rows, zeros_rows), jnp.arange(blocks, dtype=jnp.int32))
    return (query_grad.reshape(queries.shape), key_grad, value_grad)

def reference(layer_in, positions, attn_gain, w_query, w_key, w_value, w_out, mlp_gain, w_gate, w_up, w_down, grad_out):
    width = layer_in.shape[1]
    inputs_seq = layer_in.reshape(N_DP, LEN, width)
    position_seq = positions.reshape(N_DP, LEN)
    grads_seq = grad_out.reshape(N_DP, LEN, width)
    gain_one = attn_gain.astype(jnp.float32)
    gain_two = mlp_gain.astype(jnp.float32)
    token_index = jnp.arange(LEN, dtype=jnp.int32)
    group_size = H // KV

    def per_sequence(carry, operands):
        seq_in, seq_pos, seq_grad = operands
        doc_starts = token_index - seq_pos
        cosine_table, sine_table = rotary_tables(seq_pos, HD)
        input_float = seq_in.astype(jnp.float32)
        inverse_one = lax.rsqrt(lax.optimization_barrier(jnp.mean(input_float * input_float, axis=-1, keepdims=True)) + epsilon)
        normed_one = input_float * inverse_one
        normed_in = (normed_one * gain_one).astype(jnp.bfloat16)
        query_pre = matmul(normed_in, w_query).reshape(LEN, H, HD)
        key_pre = matmul(normed_in, w_key).reshape(LEN, KV, HD)
        value_pre = matmul(normed_in, w_value).reshape(LEN, KV, HD)
        queries = rotate(query_pre, cosine_table, sine_table).astype(jnp.bfloat16).reshape(LEN, KV, group_size, HD)
        key_rows = rotate(key_pre, cosine_table, sine_table).astype(jnp.bfloat16)
        value_rows = value_pre.astype(jnp.bfloat16)
        mixed_rows, log_totals = attend(queries, key_rows, value_rows, doc_starts)
        mixed_flat = mixed_rows.reshape(LEN, H * HD)
        resid = input_float + matmul(mixed_flat, w_out)
        inverse_two = lax.rsqrt(lax.optimization_barrier(jnp.mean(resid * resid, axis=-1, keepdims=True)) + epsilon)
        normed_two = resid * inverse_two
        normed_mid = (normed_two * gain_two).astype(jnp.bfloat16)
        gate_pre = matmul(normed_mid, w_gate)
        up_proj = matmul(normed_mid, w_up)
        sigmoid_gate = jax.nn.sigmoid(gate_pre)
        hidden_act = (gate_pre * sigmoid_gate * up_proj).astype(jnp.bfloat16)
        seq_out = (resid + matmul(hidden_act, w_down)).astype(jnp.bfloat16)
        grad_down_w = outer_product(hidden_act, seq_grad)
        grad_hidden = times_transpose(seq_grad, w_down)
        grad_gate_pre = (grad_hidden * up_proj * sigmoid_gate * (1.0 + gate_pre * (1.0 - sigmoid_gate))).astype(jnp.bfloat16)
        grad_up_proj = (grad_hidden * gate_pre * sigmoid_gate).astype(jnp.bfloat16)
        grad_gate_w = outer_product(normed_mid, grad_gate_pre)
        grad_up_w = outer_product(normed_mid, grad_up_proj)
        grad_mid = times_transpose(grad_gate_pre, w_gate) + times_transpose(grad_up_proj, w_up)
        grad_gain_two = lax.optimization_barrier(jnp.sum(grad_mid * normed_two, axis=0))
        grad_resid = seq_grad.astype(jnp.float32) + norm_backward(grad_mid * gain_two, normed_two, inverse_two)
        resid_rounded = grad_resid.astype(jnp.bfloat16)
        grad_out_w = outer_product(mixed_flat, resid_rounded)
        grad_mixed = times_transpose(resid_rounded, w_out).astype(jnp.bfloat16).reshape(LEN, KV, group_size, HD)
        query_grad, key_grad, value_grad = attend_back(queries, key_rows, value_rows, grad_mixed, log_totals, doc_starts)
        query_back = unrotate(query_grad.reshape(LEN, H, HD), cosine_table, sine_table).astype(jnp.bfloat16).reshape(LEN, H * HD)
        key_back = unrotate(key_grad, cosine_table, sine_table).astype(jnp.bfloat16).reshape(LEN, KV * HD)
        value_back = value_grad.astype(jnp.bfloat16).reshape(LEN, KV * HD)
        grad_query_w = outer_product(normed_in, query_back)
        grad_key_w = outer_product(normed_in, key_back)
        grad_value_w = outer_product(normed_in, value_back)
        grad_first = times_transpose(query_back, w_query) + times_transpose(key_back, w_key) + times_transpose(value_back, w_value)
        grad_gain_one = lax.optimization_barrier(jnp.sum(grad_first * normed_one, axis=0))
        grad_input = grad_resid + norm_backward(grad_first * gain_one, normed_one, inverse_one)
        terms = (grad_gain_one, grad_query_w, grad_key_w, grad_value_w, grad_out_w, grad_gain_two, grad_gate_w, grad_up_w, grad_down_w)
        carry = tuple((total + term for total, term in zip(carry, terms)))
        return (carry, (seq_out, grad_input))
    start_carry = (jnp.zeros((width,), jnp.float32), jnp.zeros(w_query.shape, jnp.float32), jnp.zeros(w_key.shape, jnp.float32), jnp.zeros(w_value.shape, jnp.float32), jnp.zeros(w_out.shape, jnp.float32), jnp.zeros((width,), jnp.float32), jnp.zeros(w_gate.shape, jnp.float32), jnp.zeros(w_up.shape, jnp.float32), jnp.zeros(w_down.shape, jnp.float32))
    sums, (outputs, input_grads) = lax.scan(per_sequence, start_carry, (inputs_seq, position_seq, grads_seq))
    return (outputs.reshape(N_DP * LEN, width), input_grads.reshape(N_DP * LEN, width), sums[0], sums[1], sums[2], sums[3], sums[4], sums[5], sums[6], sums[7], sums[8])
```

```python
import functools

import jax
import jax.numpy as jnp
from jax import lax
from jax.experimental import pallas as pl
from jax.experimental.pallas import tpu as pltpu
from jax.sharding import PartitionSpec as P

HD = 64
EPS = 1e-05
ROPE_BASE = 500000.0
F32 = jnp.float32
BF16 = jnp.bfloat16


def matmul(left, right):
    return jnp.dot(left, right, preferred_element_type=F32)


def outer_product(left, right):
    return lax.dot_general(left, right, (((0,), (0,)), ((), ())), preferred_element_type=F32)


def times_transpose(left, right):
    return lax.dot_general(left, right, (((1,), (1,)), ((), ())), preferred_element_type=F32)


def norm_backward(grad_normed, normed, inverse_rms):
    return inverse_rms * (
        grad_normed - normed * jnp.mean(grad_normed * normed, axis=-1, keepdims=True)
    )


def tie(value, *others):
    return lax.optimization_barrier((value, *others))[0]


def tie_all(values, *others):
    return lax.optimization_barrier((*values, *others))[: len(values)]


def pick(bit, zero, one):
    return jnp.where(bit == 0, zero, one)


def in_order(bit, own, got, axis=0):
    return jnp.stack([pick(bit, own, got), pick(bit, got, own)], axis=axis)


def half_of(bit, array, axis):
    return pick(bit, lax.index_in_dim(array, 0, axis, False), lax.index_in_dim(array, 1, axis, False))


def place_kernel(moves, n_in, n_out, index, *refs):
    ins, outs = refs[:n_in], refs[n_in : n_in + n_out]
    scratch, in_sem, out_sem = refs[n_in + n_out :]
    loads, stores = [], []
    for i, (a, source, o, slot, target) in enumerate(moves):
        held = scratch.at[slot]
        loads.append(pltpu.make_async_copy(ins[a].at[source], held, in_sem.at[i]))
        stores.append(pltpu.make_async_copy(held, outs[o].at[target(index)], out_sem.at[i]))
    for load in loads:
        load.start()
    for load, store in zip(loads, stores):
        load.wait()
        store.start()
    for store in stores:
        store.wait()


def place(arrays, shapes, moves, piece, index):
    hbm = pl.BlockSpec(memory_space=pl.ANY)
    dtype = arrays[0].dtype
    moves = [(a, s, o, i, t) for i, (a, s, o, t) in enumerate(moves)]
    size = sum(v.size for v in arrays) * 2
    return pl.pallas_call(
        functools.partial(place_kernel, moves, len(arrays), len(shapes)),
        out_shape=[jax.ShapeDtypeStruct(s, dtype) for s in shapes],
        in_specs=[pl.BlockSpec(memory_space=pltpu.SMEM)] + [hbm] * len(arrays),
        out_specs=[hbm] * len(shapes),
        scratch_shapes=[
            pltpu.VMEM((len(moves), *piece), dtype),
            pltpu.SemaphoreType.DMA((len(moves),)),
            pltpu.SemaphoreType.DMA((len(moves),)),
        ],
        cost_estimate=pl.CostEstimate(flops=0, bytes_accessed=2 * size, transcendentals=0),
        name="place",
    )(index, *arrays)


def join(pieces):
    rows, width = pieces[0].shape[-2:]
    moves, at = [], 0
    for a, p in enumerate(pieces):
        for k in range(p.size // (rows * width)):
            source = (k,) if p.ndim == 3 else (slice(None),)
            moves.append((a, source, 0, lambda _, at=at: (pl.ds(at, rows),)))
            at += rows
    return place(pieces, [(at, width)], moves, (rows, width), jnp.zeros((1,), jnp.int32))[0]


LANES = 128


def half_turn(v):
    lane = lax.broadcasted_iota(jnp.int32, v.shape, 1)
    return jnp.where(lane % HD < HD // 2, pltpu.roll(v, LANES - HD // 2, 1), pltpu.roll(v, HD // 2, 1))


def turn_heads(v, cosine, sine, n_rope):
    out = []
    for i in range(0, v.shape[1], LANES):
        part = v[:, i : i + LANES]
        lane = lax.broadcasted_iota(jnp.int32, part.shape, 1) + i
        turned = part * cosine + half_turn(part) * sine
        out.append(jnp.where(lane < n_rope, turned, part))
    return jnp.concatenate(out, axis=1)


def project_kernel(n_pieces, n_weights, n_rope, blk, offs, *refs):
    pieces, weights = refs[:n_pieces], refs[n_pieces : n_pieces + n_weights]
    cos_ref, sin_ref, h_ref, out_ref, gain_ref = refs[n_pieces + n_weights :]
    for r, w in enumerate(weights):
        at = pl.ds(pl.multiple_of(offs[r], blk), blk)
        gain_ref[0:1, at] = w[blk : blk + 1, :blk].astype(F32)
        gain_ref[1:2, at] = w[blk + 1 : blk + 2, :blk].astype(F32)
    rows = pieces[0].shape[0]
    for i in range(0, n_pieces, 2):
        for j in (i, i + 1):
            v = pieces[j][...].astype(F32)
            inverse = lax.rsqrt(jnp.mean(v * v, axis=-1, keepdims=True) + EPS)
            h_ref[j * rows : (j + 1) * rows, :] = (v * inverse * gain_ref[0:1, :]).astype(BF16)
        at = slice(i * rows, (i + 2) * rows)
        total = jnp.zeros((2 * rows, out_ref.shape[1]), F32)
        for r, w in enumerate(weights):
            h = h_ref[at, pl.ds(pl.multiple_of(offs[r], blk), blk)]
            total = total + jnp.dot(h, w[:blk, :], preferred_element_type=F32)
        out_ref[at, :] = turn_heads(total, cos_ref[at, :], sin_ref[at, :], n_rope).astype(BF16)


def project(pieces, weights, offs, cosine, sine, n_rope):
    rows, width = pieces[0].shape
    blk, n = weights[0].shape[0] - 16, weights[0].shape[1]
    total = rows * len(pieces)
    vmem = pl.BlockSpec(memory_space=pltpu.VMEM)
    return pl.pallas_call(
        functools.partial(project_kernel, len(pieces), len(weights), n_rope, blk),
        out_shape=(
            jax.ShapeDtypeStruct((total, width), BF16),
            jax.ShapeDtypeStruct((total, n), BF16),
            jax.ShapeDtypeStruct((2, width), F32),
        ),
        in_specs=[pl.BlockSpec(memory_space=pltpu.SMEM)] + [vmem] * (len(pieces) + len(weights) + 2),
        out_specs=(vmem, vmem, vmem),
        cost_estimate=pl.CostEstimate(
            flops=2 * total * width * n, bytes_accessed=4 * total * width, transcendentals=0
        ),
        name="project",
    )(offs, *pieces, *weights, cosine, sine)


def dot_nt(a, b):
    return lax.dot_general(a, b, (((1,), (1,)), ((), ())), preferred_element_type=F32)


def masked(k, q, tok_col, tok_row, start_col, start_row):
    s = dot_nt(k, q) * HD ** (-0.5)
    allowed = (tok_col <= tok_row) & (start_col == start_row)
    return jnp.where(allowed, s, -jnp.inf)


def attend_kernel(per, qkv_ref, tok_col, tok_row, start_col, start_row, mixed_ref, lse_ref):
    n_q = per * HD
    seq = tok_row.shape[-1]
    qkv = qkv_ref[...].reshape(seq, qkv_ref.shape[-1])
    k, v = qkv[:, n_q : n_q + HD], qkv[:, n_q + HD :]
    v_t = v.T
    outs = []
    for j in range(per):
        q = qkv[:, j * HD : (j + 1) * HD]
        s = masked(k, q, tok_col[...], tok_row[...], start_col[0], start_row[0])
        top = jnp.max(s, axis=0, keepdims=True)
        e = jnp.exp(s - top)
        total = jnp.sum(e, axis=0, keepdims=True)
        p = (e / total).astype(BF16)
        outs.append(jnp.dot(v_t, p, preferred_element_type=F32))
        lse_ref[0, j : j + 1, :] = top + jnp.log(total)
    mixed = jnp.concatenate(outs, axis=0).T.astype(BF16)
    mixed_ref[...] = mixed.reshape(mixed_ref.shape)


def attend_back_kernel(
    per, qkv_ref, dm_ref, lse_ref, tok_col, tok_row, start_col, start_row, cos_ref, sin_ref, out_ref
):
    n_q = per * HD
    seq = tok_row.shape[-1]
    qkv = qkv_ref[...].reshape(seq, qkv_ref.shape[-1])
    dm = dm_ref[...].reshape(seq, n_q)
    k, v = qkv[:, n_q : n_q + HD], qkv[:, n_q + HD :]
    k_t = k.T
    dqs = []
    dk = jnp.zeros((seq, HD), F32)
    dv = jnp.zeros((seq, HD), F32)
    for j in range(per):
        q, d = qkv[:, j * HD : (j + 1) * HD], dm[:, j * HD : (j + 1) * HD]
        s = masked(k, q, tok_col[...], tok_row[...], start_col[0], start_row[0])
        p = jnp.exp(s - lse_ref[0, j : j + 1, :])
        dprob = dot_nt(v, d)
        delta = jnp.sum(p * dprob, axis=0, keepdims=True)
        ds = (p * (dprob - delta)).astype(BF16)
        dqs.append(jnp.dot(k_t, ds, preferred_element_type=F32))
        dk = dk + jnp.dot(ds, q, preferred_element_type=F32)
        dv = dv + jnp.dot(p.astype(BF16), d, preferred_element_type=F32)
    scale = HD ** (-0.5)
    dq = jnp.concatenate(dqs, axis=0).T * scale
    out = jnp.concatenate([dq, dk * scale, dv], axis=1)
    cosine, sine = cos_ref[...].reshape(seq, LANES), sin_ref[...].reshape(seq, LANES)
    out_ref[...] = turn_heads(out, cosine, -sine, n_q + HD).astype(BF16).reshape(out_ref.shape)


def attention_specs(seq, per):
    n_q = per * HD

    def tokens(n):
        return pl.BlockSpec((2, 1, seq // 2, n), lambda s: (0, s, 0, 0))

    vectors = [
        pl.BlockSpec((seq, 1), lambda s: (0, 0)),
        pl.BlockSpec((1, seq), lambda s: (0, 0)),
        pl.BlockSpec((1, seq, 1), lambda s: (s, 0, 0)),
        pl.BlockSpec((1, 1, seq), lambda s: (s, 0, 0)),
    ]
    return tokens(n_q), tokens(n_q + 2 * HD), tokens(LANES), pl.BlockSpec((1, per, seq), lambda s: (s, 0, 0)), vectors


def attend(qkv, vectors, per):
    seq = vectors[1].shape[-1]
    q_spec, qkv_spec, _, lse_spec, vector_specs = attention_specs(seq, per)
    mixed, lse = pl.pallas_call(
        functools.partial(attend_kernel, per),
        grid=(2,),
        out_shape=(
            jax.ShapeDtypeStruct((2, 2, seq // 2, per * HD), BF16),
            jax.ShapeDtypeStruct((2, per, seq), F32),
        ),
        in_specs=[qkv_spec, *vector_specs],
        out_specs=(q_spec, lse_spec),
        cost_estimate=pl.CostEstimate(
            flops=8 * per * seq * seq * HD, bytes_accessed=8 * seq * per * HD, transcendentals=2 * per * seq * seq
        ),
        name="attend",
    )(qkv.reshape(2, 2, seq // 2, -1), *vectors)
    return mixed.reshape(2 * seq, per * HD), lse


def attend_back(qkv, dmixed, lse, vectors, cosine, sine, per):
    seq = vectors[1].shape[-1]
    q_spec, qkv_spec, table_spec, lse_spec, vector_specs = attention_specs(seq, per)
    out = pl.pallas_call(
        functools.partial(attend_back_kernel, per),
        grid=(2,),
        out_shape=jax.ShapeDtypeStruct((2, 2, seq // 2, (per + 2) * HD), BF16),
        in_specs=[qkv_spec, q_spec, lse_spec, *vector_specs, table_spec, table_spec],
        out_specs=qkv_spec,
        cost_estimate=pl.CostEstimate(
            flops=20 * per * seq * seq * HD, bytes_accessed=16 * seq * per * HD, transcendentals=2 * per * seq * seq
        ),
        name="attend_back",
    )(*[v.reshape(2, 2, seq // 2, -1) for v in (qkv, dmixed)], lse, *vectors, *[v.reshape(2, 2, seq // 2, -1) for v in (cosine, sine)])
    return out.reshape(2 * seq, -1)


def layer(
    n_dp,
    n_t,
    layer_in,
    positions,
    attn_gain,
    w_query,
    w_key,
    w_value,
    w_out,
    mlp_gain,
    w_gate,
    w_up,
    w_down,
    grad_out,
):
    n = n_dp * n_t
    dp, t = lax.axis_index("dp"), lax.axis_index("tensor")
    c, y, x = t % 2, t // 2, dp % 2
    dp_bits = n_dp.bit_length() - 1
    h = dp // (n_dp // 2)
    C, Y, X, H = 1, 2, n_t, n // 2
    l_bits = [((dp // (1 << k)) % 2, n_t << k) for k in range(1, dp_bits - 1)]
    n_l = n_dp // 4
    seq = positions.shape[0]
    rows, width = layer_in.shape
    blk = width // n_dp

    def swap(value, mask):
        return lax.ppermute(value, ("dp", "tensor"), [(i, i ^ mask) for i in range(n)])

    def near4(v):
        return [v, swap(v, Y), swap(v, X), swap(v, X | Y)]

    def with_core(pieces):
        return [*pieces, *(swap(p, C) for p in pieces)]

    def chip_sum(v):
        got = swap(v[4 * rows :], C)
        return [v[i : i + rows].astype(F32) + got[i : i + rows].astype(F32) for i in range(0, 4 * rows, rows)]

    def send3(near):
        return [swap(p.astype(BF16), m) for p, m in zip(near[1:], (Y, X, X | Y))]

    def total(own, parts):
        return own + sum(p.astype(F32) for p in parts)

    def scatter_l(v, *after):
        for bit, mask in reversed(l_bits):
            v = v.reshape(2, 2, v.shape[1] // 2, *v.shape[2:])
            got = swap(half_of(1 - bit, v, 1).astype(BF16), mask)
            v = half_of(bit, v, 1).astype(F32) + tie(got, *after).astype(F32)
        return v[:, 0]

    def trade(v, bit, mask, *first):
        keep, sent = half_of(bit, v, 0), half_of(1 - bit, v, 0).astype(BF16)
        got = swap(tie(sent, *first), mask)
        return in_order(bit, keep, got.astype(F32)), got

    n_q, n_k = w_query.shape[1] // 2, w_key.shape[1] // 2
    n_qkv = n_q + 2 * n_k
    heads = n_q // HD
    gains = jnp.pad(jnp.stack([attn_gain, mlp_gain]), ((0, 14), (0, n_qkv - blk)))

    def qkv_half(i):
        own = [w[:, i * m : (i + 1) * m] for w, m in ((w_query, n_q), (w_key, n_k), (w_value, n_k))]
        return jnp.concatenate([jnp.concatenate(own, axis=1), gains])

    qkv_halves = (qkv_half(0), qkv_half(1))
    qkv_same, qkv_other = pick(x, *qkv_halves), pick(1 - x, *qkv_halves)
    qkv_pieces = [
        qkv_same if r == 0 else swap(qkv_other if r % 2 else qkv_same, n_t * r) for r in range(n_dp)
    ]
    token_near = near4(layer_in)
    token_pieces = with_core(token_near)
    far_positions = swap(tie(positions, token_near[1]), X)

    def block_at(r):
        return dp ^ r

    def merged(pieces):
        size, offs = blk, [block_at(r) * blk for r in range(n_dp)]
        if size % LANES == 0:
            return pieces, offs
        out = []
        for r in range(0, n_dp, 2):
            a, b = pick(x, pieces[r], pieces[r + 1]), pick(x, pieces[r + 1], pieces[r])
            gain = jnp.concatenate([a[size : size + 2, :size], b[size : size + 2, :size]], axis=1)
            gain = jnp.pad(gain, ((0, 14), (0, n_qkv - 2 * size)))
            out.append(jnp.concatenate([a[:size], b[:size], gain]))
        return out, [block_at(r) // 2 * 2 * size for r in range(0, n_dp, 2)]

    ff = w_gate.shape[1] // 4

    def exchange(parts, *first):
        def part(dx, dh):
            return pick(x ^ dx, *(pick(h ^ dh, *parts[i]) for i in (0, 1)))

        masks = ((0, 0, 0), (X, 1, 0), (H, 0, 1), (X | H, 1, 1))
        return [swap(tie(part(a, b), *first), m) if m else part(a, b) for m, a, b in masks]

    def over_l(pieces):
        out = [join(pieces)]
        for _, mask in l_bits:
            out = [*out, *(swap(v, mask) for v in out)]
        return out

    def offsets(scale):
        return jnp.stack(
            [
                block_at(dx + 2 * dl + (n_dp // 2) * dh) * scale
                for dl in range(n_l)
                for dh in (0, 1)
                for dx in (0, 1)
            ]
        ).astype(jnp.int32)

    def place_rows(arrays, k, splits):
        m = arrays[0].shape[1]
        part = m // splits
        moves = []
        for a in range(n_l):
            for i in range(4):
                for s in range(splits):
                    moves.append(
                        (
                            a,
                            (pl.ds(i * k, k), pl.ds(s * part, part)),
                            s,
                            lambda index, j=4 * a + i: (pl.ds(pl.multiple_of(index[j], k), k),),
                        )
                    )
        return place(arrays, [(width, part)] * splits, moves, (k, part), offsets(k))

    def place_columns(arrays, k):
        if blk % LANES:
            order = jnp.concatenate([v.reshape(4, k, blk) for v in arrays])
            slots = offsets(1)
            back = jnp.zeros((n_dp,), jnp.int32).at[slots].set(jnp.arange(n_dp, dtype=jnp.int32))
            return jnp.moveaxis(order[back], 0, 1).reshape(k, width)
        moves = [
            (
                a,
                (pl.ds(i * k, k),),
                0,
                lambda index, j=4 * a + i: (slice(None), pl.ds(pl.multiple_of(index[j], blk), blk)),
            )
            for a in range(n_l)
            for i in range(4)
        ]
        return place(arrays, [(k, width)], moves, (k, blk), offsets(blk))[0]

    wo_half = w_out.shape[0] // 2
    early = (qkv_same, qkv_other)

    def first_of(w, i, j, k):
        return w[:, (2 * i + j) * k : (2 * i + j + 1) * k]

    wo_parts = [[w_out[i * wo_half : (i + 1) * wo_half]] * 2 for i in (0, 1)]
    wo_pieces = exchange(wo_parts, token_near[1], *early)
    gu_parts = [
        [jnp.concatenate([first_of(w_gate, i, j, ff), first_of(w_up, i, j, ff)], axis=1) for j in (0, 1)]
        for i in (0, 1)
    ]
    gu_pieces = exchange(gu_parts, token_near[2], token_near[3])
    d_parts = [[w_down[(2 * i + j) * ff : (2 * i + j + 1) * ff] for j in (0, 1)] for i in (0, 1)]
    d_pieces = exchange(d_parts, *qkv_pieces[1:])
    far_grad = swap(tie(grad_out, *qkv_pieces[1:]), H)
    grad_x = swap(tie(grad_out, *qkv_pieces[1:]), X)

    def relative(v):
        v = v.reshape(2, 2, rows).swapaxes(0, 1)
        v = jnp.stack([half_of(c, v, 0), half_of(1 - c, v, 0)])
        return jnp.stack([half_of(y, v, 1), half_of(1 - y, v, 1)], axis=1).reshape(seq)

    token = relative(jnp.arange(seq, dtype=jnp.int32))
    pos_two = jnp.stack([relative(positions), relative(far_positions)])
    starts = token[None] - pos_two
    vectors = (token[:, None], token[None], starts[:, :, None], starts[:, None, :])
    pos_dev = jnp.swapaxes(pos_two.reshape(2, 2, 2 * rows), 0, 1).reshape(2 * seq)
    inverse = ROPE_BASE ** (-2.0 * jnp.arange(HD // 2, dtype=F32) / HD)
    angles = pos_dev.astype(F32)[:, None] * inverse[None, :]
    cosine, sine = jnp.cos(angles), jnp.sin(angles)
    cosine = jnp.concatenate([cosine] * 4, axis=1)
    sine = jnp.concatenate([-sine, sine, -sine, sine], axis=1)

    weights, offs = merged(qkv_pieces)
    h1, qkv, gain_rows = project(
        token_pieces, weights, jnp.stack(offs).astype(jnp.int32), cosine, sine, n_q + n_k
    )
    gain_one, gain_two = gain_rows[0], gain_rows[1]
    wo_all = over_l([tie(p, qkv) for p in wo_pieces])
    mixed, lse = attend(tie(qkv, wo_all[0]), vectors, heads)
    w_o = place_columns([tie(v, mixed) for v in wo_all], wo_half)
    w_qkv_ordered = place(
        [tie(p, mixed) for p in qkv_pieces],
        [(width, n_qkv)],
        [
            (r, (pl.ds(0, blk),), 0, lambda index, r=r: (pl.ds(pl.multiple_of(index[r], blk), blk),))
            for r in range(n_dp)
        ],
        (blk, n_qkv),
        jnp.stack([block_at(r) * blk for r in range(n_dp)]).astype(jnp.int32),
    )[0]
    out_near = chip_sum(matmul(mixed, w_o).astype(BF16))
    out_parts = send3(out_near)

    sent = [p.astype(BF16) for p in out_near[1:]]
    gu_all = over_l([tie(p, *sent) for p in gu_pieces])
    grad_pair = join([tie(grad_out, gu_all[0]), grad_x])
    grad_y = swap(grad_pair, Y)

    input_float = layer_in.astype(F32)
    inverse_one = lax.rsqrt(jnp.mean(input_float * input_float, axis=-1, keepdims=True) + EPS)
    normed_one = input_float * inverse_one
    resid = input_float + total(out_near[0], [tie(p, grad_pair) for p in out_parts])

    inverse_two = lax.rsqrt(jnp.mean(resid * resid, axis=-1, keepdims=True) + EPS)
    normed_two = resid * inverse_two
    mid = (normed_two * gain_two).astype(BF16)
    far_mid = swap(mid, H)
    mid_near = near4(mid)
    far_grad_x = swap(tie(far_grad, mid), X)
    d_all = over_l([tie(p, mid) for p in d_pieces])
    w_g, w_u = place_rows([tie(v, d_all[0]) for v in gu_all], blk, 2)
    h2_near = join(with_core(mid_near))
    far_near = near4(far_mid)
    far_grad_y = swap(join([tie(far_grad, far_mid), far_grad_x]), Y)
    w_d = place_columns([tie(v, w_g) for v in d_all], ff)

    def four(own, over_x, pair):
        return [own, pair[:rows], over_x, pair[rows:]]

    grad_near = join(with_core(four(grad_out, grad_x, grad_y)))
    h2_far = join(with_core(far_near))
    grad_far = join(with_core(four(far_grad, far_grad_x, far_grad_y)))

    def mlp(h2, grad):
        gate_pre, up_proj = matmul(h2, w_g), matmul(h2, w_u)
        sig = jax.nn.sigmoid(gate_pre)
        hidden = (gate_pre * sig * up_proj).astype(BF16)
        grad_hidden = times_transpose(grad, w_d)
        dgate = (grad_hidden * up_proj * sig * (1.0 + gate_pre * (1.0 - sig))).astype(BF16)
        dup = (grad_hidden * gate_pre * sig).astype(BF16)
        part = times_transpose(dgate, w_g) + times_transpose(dup, w_u)
        return hidden, dgate, dup, part.astype(BF16)

    hidden0, dgate0, dup0, mid0 = mlp(h2_near, grad_near)
    near_sum = chip_sum(mid0)
    near_parts = send3(near_sum)
    hidden1, dgate1, dup1, mid1 = mlp(tie(h2_far, near_sum[1]), grad_far)
    far_sum = chip_sum(mid1)
    far_parts = send3(far_sum)

    hidden_all = tie(jnp.concatenate([hidden0, hidden1]), *far_sum)
    dgate_all, dup_all = jnp.concatenate([dgate0, dgate1]), jnp.concatenate([dup0, dup1])
    h2_all, grad_all = jnp.concatenate([h2_near, h2_far]), jnp.concatenate([grad_near, grad_far])
    g_d = outer_product(hidden_all, grad_all)
    g_g = outer_product(tie(h2_all, g_d), dgate_all)
    far_total = total(far_sum[0], [tie(p, g_g) for p in far_parts])
    far_dh2 = swap(far_total.astype(BF16), H)
    g_u = outer_product(h2_all, tie(dup_all, far_total))
    out_part = matmul(tie(hidden_all, g_u), w_d).astype(BF16)
    near_total = total(near_sum[0], [tie(p, out_part) for p in near_parts])
    dh2 = near_total + far_dh2.astype(F32)

    dresid = grad_out.astype(F32) + norm_backward(dh2 * gain_two, normed_two, inverse_two)
    dresid_near = near4(dresid.astype(BF16))

    def by_block(g):
        return jnp.stack(jnp.split(g, n_dp, axis=1)).reshape(2, n_l, 2, g.shape[0], blk)

    d_sum, d_two = trade(scatter_l(by_block(g_d), dresid), h, H, dresid)
    g_sum, g_two = trade(scatter_l(g_g.reshape(2, n_l, 2, blk, ff), d_sum), h, H, d_sum)
    u_sum, u_two = trade(scatter_l(g_u.reshape(2, n_l, 2, blk, ff), g_sum), h, H, g_sum)
    dresid_b = join(with_core([dresid_near[0], *(tie(p, g_two) for p in dresid_near[1:])]))

    dmixed = times_transpose(dresid_b, w_o).astype(BF16)
    dqkv = attend_back(qkv, dmixed, lse, vectors, cosine, sine, heads)
    g_qkv = outer_product(h1, dqkv)
    dh1_near = chip_sum(times_transpose(tie(dqkv, g_qkv), w_qkv_ordered).astype(BF16))
    dh1_parts = send3(dh1_near)
    g_o = outer_product(mixed, tie(dresid_b, *dh1_near))

    qkv_part = scatter_l(g_qkv.reshape(2, n_l, 2, blk, n_qkv), g_o)

    def scatter_h(v):
        return half_of(h, v, 0) + swap(half_of(1 - h, v, 0).astype(BF16), H).astype(F32)

    qkv_sum = trade(scatter_h(qkv_part), x, X)[0]
    o_sum = scatter_h(scatter_l(by_block(g_o), qkv_part))
    out_sum = trade(o_sum, x, X)[0].reshape(2 * n_q, blk)

    def chip_sums_slow(v, *first):
        near = chip_sum(tie(v, *first))
        pair = jnp.concatenate([near[1].astype(BF16), near[3].astype(BF16)])
        return near, pair

    o_near, o_near_pair = chip_sums_slow(out_part[: 8 * rows], dmixed)
    o_far, o_far_pair = chip_sums_slow(out_part[8 * rows :], dmixed)
    got_far = swap(tie(o_far_pair, dresid_b), Y)
    got_near = swap(tie(o_near_pair, dresid_b), Y)
    d_sum = trade(jnp.swapaxes(d_sum, 0, 1), x, X, dresid_b)[0]
    g_sum = trade(jnp.swapaxes(g_sum, 0, 1), x, X, dresid_b)[0]
    u_sum = trade(jnp.swapaxes(u_sum, 0, 1), x, X, dresid_b)[0]

    def finish_slow(near, got):
        return near[0] + got[:rows].astype(F32) + swap((near[2] + got[rows:]).astype(BF16), X).astype(F32)

    got_far, got_near = tie(got_far, *dh1_near), tie(got_near, *dh1_near)
    o_far_total = swap(finish_slow(o_far, got_far).astype(BF16), H)
    layer_out = (resid + finish_slow(o_near, got_near) + o_far_total.astype(F32)).astype(BF16)

    dh1 = total(dh1_near[0], dh1_parts)
    grad_in = dresid + norm_backward(dh1 * gain_one, normed_one, inverse_one)

    down_sum = d_sum.reshape(4 * ff, blk)

    def wide(v):
        return jnp.concatenate([v[0, 0], v[0, 1], v[1, 0], v[1, 1]], axis=1)

    gate_sum, up_sum = wide(g_sum), wide(u_sum)

    def both_x(first, last):
        return jnp.concatenate([qkv_sum[0, :, first:last], qkv_sum[1, :, first:last]], axis=1)

    query_sum, key_sum = both_x(0, n_q), both_x(n_q, n_q + n_k)
    value_sum = both_x(n_q + n_k, n_qkv)

    def dots(g, w):
        return jnp.sum(g * w.astype(F32), axis=-1)

    w_mine = w_qkv_ordered.reshape(2, n_l, 2, blk, n_qkv)
    for bit, _ in reversed(l_bits):
        w_mine = half_of(bit, w_mine.reshape(2, 2, w_mine.shape[1] // 2, *w_mine.shape[2:]), 1)
    term = dots(qkv_part, w_mine[:, 0])
    for mask in (C, Y):
        term = term + swap(term, mask)
    term = half_of(h, term, 0) + swap(half_of(1 - h, term, 0), H)
    term = half_of(x, term, 0) + swap(half_of(1 - x, term, 0), X)
    gain_one_sum = term / attn_gain.astype(F32)
    term = dots(gate_sum, w_gate) + dots(up_sum, w_up)
    for mask in (C, Y):
        term = term + swap(term, mask)
    gain_two_sum = term / mlp_gain.astype(F32)
    return (
        layer_out,
        grad_in,
        gain_one_sum,
        query_sum,
        key_sum,
        value_sum,
        out_sum,
        gain_two_sum,
        gate_sum,
        up_sum,
        down_sum,
    )


def solution(mesh):
    tokens = P(("dp", "tensor"), None)
    columns, rows, one = P("dp", "tensor"), P("tensor", "dp"), P("dp")
    return jax.shard_map(
        functools.partial(layer, mesh.shape["dp"], mesh.shape["tensor"]),
        mesh=mesh,
        in_specs=(
            tokens,
            one,
            one,
            columns,
            columns,
            columns,
            rows,
            one,
            columns,
            columns,
            rows,
            tokens,
        ),
        out_specs=(
            tokens,
            tokens,
            one,
            columns,
            columns,
            columns,
            rows,
            one,
            columns,
            columns,
            rows,
        ),
        check_vma=False,
    )
```
